256 devices in a mesh: chan: 32 (over x, z), win: 8 (over y, core).
Axes of the slice: x: 4, y: 4, z: 8, core: 2. Of those that a mesh axis runs over, the one named last changes fastest.
Arguments:
- spectra: bfloat16 [2, 16, 2048, 1024], P(None, 'win', 'chan'), may hold values from -200 to 200
- pair_blocks: int32 [256, 2], P(('chan', 'win')), may hold values from 0 to 31, as said below
Outputs:
- stacks: float32 [256, 64, 64, 256], P(('chan', 'win'))
The draws below stay inside these ranges and needn't reach their ends.
Inputs may be any that keep to these rules, and one draw needn't show every extreme that they name: `pair_blocks`: row p belongs to channel block c = p // 8. The 8 rows of c hold, in a drawn order and each in a drawn orientation, the pairs of blocks c - d // 2 and c - d // 2 + d for d = 0 to 7, block numbers taken modulo 32; so every pair of blocks at cyclic distance below 8 appears exactly once in all.
All inputs are finite; a program needn't handle non-finite values.
Results may differ from the reference program's by a relative error of at most 0.0032.
Values may be sent and summed in bfloat16 or wider, within the bound.
No kernel may reach another device: no remote copies, remote signals or barrier semaphores. Data moves between devices by JAX's collectives and lax.ppermute only.
A program may use at most 256 MiB of HBM per device.

```python
import math
import jax
import jax.numpy as jnp
from jax import lax

CH = 64
F = 1024
NLAG = 256
BLOCKS = 32
CHANNELS = 2048
WINDOWS = 16
OWNER_ROWS = 8
NPB = 256
HALF_BAND = 64


def draw_spectra(key, part):
    key_base, key_level, key_rate, key_phase = jax.random.split(jax.random.fold_in(key, 7), 4)
    full_shape = (2, WINDOWS, CHANNELS, F)
    base = jnp.clip(jax.random.normal(key_base, full_shape, jnp.float32), -6.0, 6.0)
    level = 10.0 ** jax.random.uniform(key_level, (1, 1, CHANNELS, 1), jnp.float32, 0.0, 1.0)
    depth = 1.2
    rates = jax.random.uniform(key_rate, (1, 1, CHANNELS, 1), jnp.float32, 0.5, 3.0)
    phases = jax.random.uniform(key_phase, (1, 1, CHANNELS, 1), jnp.float32, 0.0, 2.0 * math.pi)
    bin_pos = jnp.arange(F, dtype=jnp.float32) / F
    tilt = jnp.exp(depth * jnp.sin(2.0 * math.pi * rates * bin_pos + phases))
    return (base * level * tilt).astype(jnp.bfloat16)


def draw_pair_blocks(key, part):
    key_order, key_flip = jax.random.split(jax.random.fold_in(key, 11))
    slots = jnp.arange(OWNER_ROWS, dtype=jnp.int32)
    scores = jax.random.randint(key_order, (BLOCKS, OWNER_ROWS), 0, 1048576) * OWNER_ROWS + slots[None, :]
    spacing = jnp.argsort(scores, axis=1, stable=True).astype(jnp.int32)
    owner = jnp.arange(BLOCKS, dtype=jnp.int32)[:, None]
    leading = owner - spacing // 2
    trailing = leading + spacing
    leading = jnp.mod(leading, BLOCKS).reshape(-1)
    trailing = jnp.mod(trailing, BLOCKS).reshape(-1)
    flip = jax.random.randint(key_flip, (NPB,), 0, 2)
    first = jnp.where(flip == 1, trailing, leading)
    second = jnp.where(flip == 1, leading, trailing)
    return jnp.stack([first, second], axis=1).astype(jnp.int32)


def setup_inputs(seed: int = 0) -> dict:
    arg_keys = jax.random.split(jax.random.key(seed), 3)
    spectra = draw_spectra(jax.random.fold_in(arg_keys[2], 71), 0)
    pair_blocks = draw_pair_blocks(jax.random.fold_in(arg_keys[2], 71), 0)
    return {"spectra": spectra, "pair_blocks": pair_blocks}


eps = 1e-05
first_bin = 60.0
samples = 15000.0

def smoothing(length_bins, half_width):
    indices = jnp.arange(length_bins, dtype=jnp.int32)
    return (jnp.abs(indices[:, None] - indices[None, :]) <= half_width).astype(jnp.float32)

def whiten(spectra):
    real_part = spectra[0].astype(jnp.float32)
    imag_part = spectra[1].astype(jnp.float32)
    powers = real_part * real_part + imag_part * imag_part
    smoother = smoothing(F, HALF_BAND)
    counts = lax.optimization_barrier(jnp.sum(smoother, axis=0))
    rows_flat = powers.reshape(-1, F)
    smooth = jnp.dot(rows_flat, smoother, precision=lax.Precision.HIGHEST) / counts
    factor = lax.rsqrt(smooth + eps).reshape(powers.shape)
    return jnp.stack([real_part * factor, imag_part * factor]).astype(jnp.bfloat16)

def make_table():
    bin_freq = first_bin + jnp.arange(F, dtype=jnp.float32)
    lag_steps = jnp.arange(NLAG, dtype=jnp.float32) - NLAG // 2
    angles = 2.0 * math.pi / samples * bin_freq[:, None] * lag_steps[None, :]
    return jnp.concatenate([jnp.cos(angles), -jnp.sin(angles)], axis=0).astype(jnp.bfloat16)

def cross_spectrum(leading, trailing):
    left_side = leading.astype(jnp.float32)
    right_side = trailing.astype(jnp.float32)
    real_sum = jnp.einsum('wif,wjf->ijf', left_side[0], right_side[0]) + jnp.einsum('wif,wjf->ijf', left_side[1], right_side[1])
    imag_sum = jnp.einsum('wif,wjf->ijf', left_side[1], right_side[0]) - jnp.einsum('wif,wjf->ijf', left_side[0], right_side[1])
    return jnp.concatenate([real_sum, imag_sum], axis=2).astype(jnp.bfloat16)

def reference(spectra, pair_blocks):
    whitened = whiten(spectra)
    lag_table = make_table()
    scaling = 1.0 / math.sqrt(WINDOWS * F)

    def correlate(pair_row):
        leading = lax.dynamic_slice_in_dim(whitened, (pair_row[0] * CH).astype(jnp.int32), CH, 2)
        trailing = lax.dynamic_slice_in_dim(whitened, (pair_row[1] * CH).astype(jnp.int32), CH, 2)
        cross = cross_spectrum(leading, trailing)
        result = jnp.dot(cross.reshape(CH * CH, 2 * F), lag_table, preferred_element_type=jnp.float32)
        return result.reshape(CH, CH, NLAG) * scaling
    return lax.map(correlate, pair_blocks)
```

```python
import functools
import math

import jax
import jax.numpy as jnp
import numpy as np
from jax import lax
from jax.experimental import pallas as pl
from jax.experimental.pallas import tpu as pltpu
from jax.sharding import PartitionSpec as P

NLAG = 256
HALF_BAND = 64
EPS = 1e-05
FIRST_BIN = 60.0
SAMPLES = 15000.0
LANES = 128
VMEM_LIMIT = 56 * 1024 * 1024


def whiten_kernel(spec_ref, out_ref):
    _, windows, rows, bins = spec_ref.shape
    width = bins + LANES
    bin_pos = lax.broadcasted_iota(jnp.int32, (1, bins), 1)
    count = (
        jnp.minimum(bin_pos + HALF_BAND, bins - 1) - jnp.maximum(bin_pos - HALF_BAND, 0) + 1
    ).astype(jnp.float32)
    lane = lax.broadcasted_iota(jnp.int32, (1, LANES), 1)
    even32 = (lane // 32) % 2 == 0
    even64 = (lane // 64) % 2 == 0
    parts = {}
    for w in range(windows):
        real = spec_ref[0, w].astype(jnp.float32)
        imag = spec_ref[1, w].astype(jnp.float32)
        power = real * real + imag * imag
        padded = jnp.concatenate([power, jnp.zeros((rows, LANES), jnp.float32)], axis=1)
        total = padded
        step = 1
        while step < 2 * HALF_BAND:
            total = total + pltpu.roll(total, width - step, 1)
            step *= 2
        window_sum = pltpu.roll(total, HALF_BAND, 1) + pltpu.roll(padded, width - HALF_BAND, 1)
        factor = lax.rsqrt(window_sum[:, :bins] / count + EPS)
        parts[0, w] = real * factor
        parts[1, w] = imag * factor
    arrays = [parts[r, w] for r in range(2) for w in range(windows)]
    for b in range(bins // LANES):
        v = [a[:, b * LANES : (b + 1) * LANES] for a in arrays]
        for lo, hi in ((0, 1), (2, 3)):
            x, y = v[lo], v[hi]
            v[lo] = jnp.where(even32, x, pltpu.roll(y, 32, 1))
            v[hi] = jnp.where(even32, pltpu.roll(x, LANES - 32, 1), y)
        for lo, hi in ((0, 2), (1, 3)):
            x, y = v[lo], v[hi]
            v[lo] = jnp.where(even64, x, pltpu.roll(y, 64, 1))
            v[hi] = jnp.where(even64, pltpu.roll(x, LANES - 64, 1), y)
        for s in range(4):
            out_ref[4 * b + s] = v[s].astype(jnp.bfloat16)


def whiten(spectra):
    _, _, rows, bins = spectra.shape
    return pl.pallas_call(
        whiten_kernel,
        out_shape=jax.ShapeDtypeStruct((bins // 32, rows, LANES), jnp.bfloat16),
        compiler_params=pltpu.CompilerParams(vmem_limit_bytes=VMEM_LIMIT),
        name="whiten",
    )(spectra)


def select_kernel(idx_ref, *refs):
    count = len(refs) - 2
    blocks, out_ref, sem = refs[:count], refs[count], refs[count + 1]
    dests, slots = out_ref.shape[:2]
    for d in range(dests):
        for s in range(slots):
            for b in range(count):

                @pl.when(idx_ref[d, s] == b)
                def _():
                    pltpu.make_async_copy(blocks[b], out_ref.at[d, s], sem).start()

    pltpu.make_async_copy(out_ref, out_ref, sem).wait()


def select_blocks(slot_index, blocks):
    dests, slots = slot_index.shape
    return pl.pallas_call(
        select_kernel,
        in_specs=[pl.BlockSpec(memory_space=pltpu.SMEM)]
        + [pl.BlockSpec(memory_space=pl.ANY)] * len(blocks),
        out_specs=pl.BlockSpec(memory_space=pl.ANY),
        out_shape=jax.ShapeDtypeStruct((dests, slots) + blocks[0].shape, blocks[0].dtype),
        scratch_shapes=[pltpu.SemaphoreType.DMA],
        name="select",
    )(slot_index, *blocks)


def merge_sources(ref, slot, s, lane):
    groups = [[], [], [], []]
    even8 = (lane // 8) % 2 == 0
    even16 = (lane // 16) % 2 == 0
    for half in range(2):
        v = [ref[4 * half + k, slot, s] for k in range(4)]
        for lo, hi in ((0, 1), (2, 3)):
            x, y = v[lo], v[hi]
            v[lo] = jnp.where(even8, x, pltpu.roll(y, 8, 1))
            v[hi] = jnp.where(even8, pltpu.roll(x, LANES - 8, 1), y)
        for lo, hi in ((0, 2), (1, 3)):
            x, y = v[lo], v[hi]
            v[lo] = jnp.where(even16, x, pltpu.roll(y, 16, 1))
            v[hi] = jnp.where(even16, pltpu.roll(x, LANES - 16, 1), y)
        for h in range(4):
            groups[h].append(v[h])
    return groups


def correlate_kernel(scaling, first, last, *refs):
    if first:
        data_ref, table_ref, out_ref, acc_ref, bins_ref, cross_ref = refs
        prior_ref = None
    else:
        data_ref, table_ref, prior_ref, out_ref, acc_ref, bins_ref, cross_ref = refs
    step = pl.program_id(0)
    rows = data_ref.shape[3]
    lane = lax.broadcasted_iota(jnp.int32, (1, LANES), 1)
    low_half = lane < 64
    sign = jnp.where(low_half, -1.0, 1.0).astype(jnp.bfloat16)
    masks = [(lane % 8 == m).astype(jnp.bfloat16) for m in range(8)]

    for s in range(4):
        left = merge_sources(data_ref, 0, s, lane)
        right = merge_sources(data_ref, 1, s, lane)
        for h in range(4):
            a = jnp.concatenate(left[h], axis=1)
            b = jnp.concatenate(right[h], axis=1)
            swapped = jnp.concatenate([pltpu.roll(x, 64, 1) * sign for x in right[h]], axis=1)
            weights = jnp.concatenate([b, swapped], axis=0)
            for m in range(8):
                mask = jnp.concatenate([masks[m], masks[m]], axis=1)
                res = lax.dot_general(
                    a * mask,
                    weights,
                    (((1,), (1,)), ((), ())),
                    preferred_element_type=jnp.float32,
                )
                bins_ref[pl.ds((8 * h + m) * rows, rows), :] = res
        for p in range(rows // 2):
            x = bins_ref[pl.ds(p, 32, stride=rows), :]
            y = bins_ref[pl.ds(p + rows // 2, 32, stride=rows), :]
            real = jnp.where(low_half, x, pltpu.roll(y, 64, 1))
            imag = jnp.where(low_half, pltpu.roll(x, 64, 1), y)
            cross_ref[pl.ds(64 * s, 32), pl.ds(LANES * p, LANES)] = real.astype(jnp.bfloat16)
            cross_ref[pl.ds(64 * s + 32, 32), pl.ds(LANES * p, LANES)] = imag.astype(jnp.bfloat16)
    part = jnp.dot(table_ref[0], cross_ref[...], preferred_element_type=jnp.float32)

    @pl.when(step == 0)
    def _():
        if first:
            acc_ref[...] = part
        else:
            acc_ref[...] = prior_ref[...] + part

    @pl.when(step > 0)
    def _():
        acc_ref[...] += part

    @pl.when(step == pl.num_programs(0) - 1)
    def _():
        if last:
            for p in range(rows // 2):
                tile = acc_ref[:, pl.ds(LANES * p, LANES)].T * scaling
                out_ref[p] = tile[:rows]
                out_ref[p + rows // 2] = tile[rows:]
        else:
            out_ref[...] = acc_ref[...]


def correlate(data, table, prior, last, scaling):
    sources, slots, segments, rows, _ = data.shape
    steps = segments // 4
    first = prior is None
    acc_shape = (NLAG, rows * rows)
    full = lambda shape: pl.BlockSpec(shape, lambda i: (0,) * len(shape), pipeline_mode=pl.Buffered(1))
    in_specs = [
        pl.BlockSpec((sources, slots, 4, rows, LANES), lambda i: (0, 0, i, 0, 0)),
        pl.BlockSpec((1, NLAG, NLAG), lambda i: (i, 0, 0)),
    ]
    operands = [data, table]
    if not first:
        in_specs.append(full(acc_shape))
        operands.append(prior)
    out_shape = (rows, rows, NLAG) if last else acc_shape
    return pl.pallas_call(
        functools.partial(correlate_kernel, scaling, first, last),
        grid=(steps,),
        in_specs=in_specs,
        out_specs=full(out_shape),
        out_shape=jax.ShapeDtypeStruct(out_shape, jnp.float32),
        scratch_shapes=[
            pltpu.VMEM(acc_shape, jnp.float32),
            pltpu.VMEM((32 * rows, LANES), jnp.float32),
            pltpu.VMEM((NLAG, rows * rows), jnp.bfloat16),
        ],
        compiler_params=pltpu.CompilerParams(
            dimension_semantics=("arbitrary",), vmem_limit_bytes=VMEM_LIMIT
        ),
        name="correlate",
    )(*operands)


def make_table(length_bins):
    bin_freq = np.float32(FIRST_BIN) + np.arange(length_bins, dtype=np.float32)
    lag_steps = np.arange(NLAG, dtype=np.float32) - np.float32(NLAG // 2)
    angles = np.float32(2.0 * math.pi / SAMPLES) * bin_freq[:, None] * lag_steps[None, :]
    table = np.stack([np.cos(angles), -np.sin(angles)]).reshape(2, length_bins // LANES, 4, 32, NLAG)
    table = table.transpose(1, 4, 2, 0, 3).reshape(length_bins // LANES, NLAG, NLAG)
    return jnp.asarray(table).astype(jnp.bfloat16)


def shifted(block, axis, distance):
    devices = range(lax.axis_size(axis))
    route = [((i - distance) % len(devices), i) for i in devices]
    return lax.ppermute(block, axis, route)


def per_device(spectra, pair_blocks):
    length_bins = spectra.shape[3]
    members = lax.axis_size("win")
    block_count = lax.axis_size("chan")
    centre = lax.axis_index("chan")
    reach = pair_blocks.shape[0] * members // 2
    scaling = 1.0 / math.sqrt(spectra.shape[1] * members * length_bins)

    rows_all = lax.all_gather(pair_blocks, "win", axis=0, tiled=True)
    slot_index = jnp.mod(rows_all - centre + (reach - 1), block_count)

    own = whiten(spectra)
    below, above = own, own
    lower, upper = [], []
    for k in range(1, reach + 1):
        above = shifted(above, "chan", -1)
        upper.append(above)
        if k < reach:
            below = shifted(below, "chan", 1)
            lower.append(below)
    blocks = lower[::-1] + [own] + upper
    outgoing = select_blocks(slot_index, blocks)
    incoming = lax.all_to_all(outgoing, "win", 0, 0, tiled=True)
    table = make_table(length_bins)
    return correlate(incoming, table, None, True, scaling)[None]


def solution(mesh):
    in_specs = (P(None, "win", "chan", None), P(("chan", "win"), None))
    out_specs = P(("chan", "win"), None, None, None)
    return jax.shard_map(
        per_device, mesh=mesh, in_specs=in_specs, out_specs=out_specs, check_vma=False
    )
```

```python
import functools
import math

import jax
import jax.numpy as jnp
import numpy as np
from jax import lax
from jax.experimental import pallas as pl
from jax.experimental.pallas import tpu as pltpu
from jax.sharding import PartitionSpec as P

NLAG = 256
HALF_BAND = 64
EPS = 1e-05
FIRST_BIN = 60.0
SAMPLES = 15000.0
LANES = 128
VMEM_LIMIT = 56 * 1024 * 1024


def place(segment, sizes):
    chunk = 0
    while segment >= sizes[chunk]:
        segment -= sizes[chunk]
        chunk += 1
    return chunk, segment


def whiten_kernel(spec_ref, *out_refs):
    _, windows, rows, bins = spec_ref.shape
    width = bins + LANES
    bin_pos = lax.broadcasted_iota(jnp.int32, (1, bins), 1)
    count = (
        jnp.minimum(bin_pos + HALF_BAND, bins - 1) - jnp.maximum(bin_pos - HALF_BAND, 0) + 1
    ).astype(jnp.float32)
    lane = lax.broadcasted_iota(jnp.int32, (1, LANES), 1)
    even32 = (lane // 32) % 2 == 0
    even64 = (lane // 64) % 2 == 0
    parts = {}
    for w in range(windows):
        real = spec_ref[0, w].astype(jnp.float32)
        imag = spec_ref[1, w].astype(jnp.float32)
        power = real * real + imag * imag
        padded = jnp.concatenate([power, jnp.zeros((rows, LANES), jnp.float32)], axis=1)
        total = padded
        step = 1
        while step < 2 * HALF_BAND:
            total = total + pltpu.roll(total, width - step, 1)
            step *= 2
        window_sum = pltpu.roll(total, HALF_BAND, 1) + pltpu.roll(padded, width - HALF_BAND, 1)
        factor = lax.rsqrt(window_sum[:, :bins] / count + EPS)
        parts[0, w] = real * factor
        parts[1, w] = imag * factor
    arrays = [parts[r, w] for r in range(2) for w in range(windows)]
    for b in range(bins // LANES):
        v = [a[:, b * LANES : (b + 1) * LANES] for a in arrays]
        for lo, hi in ((0, 1), (2, 3)):
            x, y = v[lo], v[hi]
            v[lo] = jnp.where(even32, x, pltpu.roll(y, 32, 1))
            v[hi] = jnp.where(even32, pltpu.roll(x, LANES - 32, 1), y)
        for lo, hi in ((0, 2), (1, 3)):
            x, y = v[lo], v[hi]
            v[lo] = jnp.where(even64, x, pltpu.roll(y, 64, 1))
            v[hi] = jnp.where(even64, pltpu.roll(x, LANES - 64, 1), y)
        for s in range(4):
            chunk, at = place(4 * b + s, [o.shape[0] for o in out_refs])
            out_refs[chunk][at] = v[s].astype(jnp.bfloat16)


def whiten(spectra, sizes):
    rows = spectra.shape[2]
    return pl.pallas_call(
        whiten_kernel,
        out_shape=[jax.ShapeDtypeStruct((n, rows, LANES), jnp.bfloat16) for n in sizes],
        compiler_params=pltpu.CompilerParams(vmem_limit_bytes=VMEM_LIMIT),
        name="whiten",
    )(spectra)


PEERS = [(dy, dc) for dy in (0, 1, 2, 3) for dc in (0, 1)]


def peer_of(chip, core, offset):
    return (chip + offset[0]) % 4 * 2 + (core + offset[1]) % 2


def select_kernel(block_count, place_ref, idx_ref, *refs):
    blocks, outs, sem = refs[:block_count], refs[block_count:-1], refs[-1]
    member = place_ref[0]
    chip, core = member // 2, member % 2
    for out_ref, offset in zip(outs, PEERS):
        dest = peer_of(chip, core, offset)
        for s in range(2):
            wanted = idx_ref[dest, s]
            for b in range(block_count):

                @pl.when(wanted == b)
                def _():
                    pltpu.make_async_copy(blocks[b], out_ref.at[s], sem).start()

    for out_ref in outs:
        pltpu.make_async_copy(out_ref, out_ref, sem).wait()


def select_blocks(member, slot_index, blocks):
    shape = jax.ShapeDtypeStruct((2,) + blocks[0].shape, blocks[0].dtype)
    return pl.pallas_call(
        functools.partial(select_kernel, len(blocks)),
        in_specs=[pl.BlockSpec(memory_space=pltpu.SMEM)] * 2
        + [pl.BlockSpec(memory_space=pltpu.VMEM)] * len(blocks),
        out_specs=[pl.BlockSpec(memory_space=pl.ANY)] * len(PEERS),
        out_shape=[shape] * len(PEERS),
        scratch_shapes=[pltpu.SemaphoreType.DMA],
        compiler_params=pltpu.CompilerParams(vmem_limit_bytes=VMEM_LIMIT),
        name="select",
    )(member, slot_index, *blocks)


def merge_sources(refs, slot, s, lane):
    v = [ref[slot, s] for ref in refs]
    for bit, width in ((1, 4), (2, 8), (4, 16)):
        even = (lane // width) % 2 == 0
        for lo in range(8):
            if lo & bit:
                continue
            hi = lo | bit
            x, y = v[lo], v[hi]
            v[lo] = jnp.where(even, x, pltpu.roll(y, width, 1))
            v[hi] = jnp.where(even, pltpu.roll(x, LANES - width, 1), y)
    return v


def correlate_kernel(scaling, first, last, *refs):
    sources, refs = refs[:8], refs[8:]
    if first:
        table_ref, mask_ref, out_ref, acc_ref, real_ref, imag_ref, cross_ref = refs
    else:
        table_ref, mask_ref, prior_ref, out_ref, acc_ref, real_ref, imag_ref, cross_ref = refs
    step = pl.program_id(0)
    rows = sources[0].shape[2]
    half = rows // 2
    pitch = real_ref.shape[0] // 32
    lane = lax.broadcasted_iota(jnp.int32, (1, LANES), 1)
    sign = jnp.where(lane < 64, -1.0, 1.0).astype(jnp.bfloat16)
    zero = jnp.zeros((rows, LANES), jnp.bfloat16)

    for s in range(4):
        left = merge_sources(sources, 0, s, lane)
        right = merge_sources(sources, 1, s, lane)
        for h in range(8):
            a = jnp.concatenate([left[h][:half], left[h][half:]], axis=1)
            b = right[h]
            turned = pltpu.roll(b, 64, 1) * sign
            weights = jnp.concatenate(
                [
                    jnp.concatenate([b, zero], axis=1),
                    jnp.concatenate([zero, b], axis=1),
                    jnp.concatenate([turned, zero], axis=1),
                    jnp.concatenate([zero, turned], axis=1),
                ],
                axis=0,
            )
            lhs = jnp.concatenate([a * mask_ref[m] for m in range(4)], axis=0)
            res = lax.dot_general(
                lhs, weights, (((1,), (1,)), ((), ())), preferred_element_type=jnp.float32
            )
            for m in range(4):
                at = pl.ds((4 * h + m) * pitch, half)
                real_ref[at, :] = res[m * half : (m + 1) * half, :LANES]
                imag_ref[at, :] = res[m * half : (m + 1) * half, LANES:]
        for p in range(half):
            cols = pl.ds(LANES * p, LANES)
            real = real_ref[pl.ds(p, 32, stride=pitch), :]
            imag = imag_ref[pl.ds(p, 32, stride=pitch), :]
            cross_ref[pl.ds(64 * s, 32), cols] = real.astype(jnp.bfloat16)
            cross_ref[pl.ds(64 * s + 32, 32), cols] = imag.astype(jnp.bfloat16)
    part = jnp.dot(table_ref[0], cross_ref[...], preferred_element_type=jnp.float32)

    @pl.when(step == 0)
    def _():
        if first:
            acc_ref[...] = part
        else:
            acc_ref[...] = prior_ref[...] + part

    @pl.when(step > 0)
    def _():
        acc_ref[...] += part

    @pl.when(step == pl.num_programs(0) - 1)
    def _():
        if last:
            for p in range(half):
                tile = acc_ref[:, pl.ds(LANES * p, LANES)].T * scaling
                out_ref[p] = tile[:rows]
                out_ref[p + half] = tile[rows:]
        else:
            out_ref[...] = acc_ref[...]


def correlate(pieces, table, prior, last, scaling):
    _, segments, rows, _ = pieces[0].shape
    first = prior is None
    acc_shape = (NLAG, rows * rows)
    lanes = np.arange(2 * LANES) % 4
    masks = np.stack([np.tile(lanes == m, (rows // 2, 1)) for m in range(4)])
    masks = jnp.asarray(masks.astype(np.float32)).astype(jnp.bfloat16)
    full = lambda shape: pl.BlockSpec(
        shape, lambda i: (0,) * len(shape), pipeline_mode=pl.Buffered(1)
    )
    in_specs = [pl.BlockSpec((2, 4, rows, LANES), lambda i: (0, i, 0, 0))] * len(pieces)
    in_specs += [pl.BlockSpec((1, NLAG, NLAG), lambda i: (i, 0, 0)), full(masks.shape)]
    operands = list(pieces) + [table, masks]
    if not first:
        in_specs.append(full(acc_shape))
        operands.append(prior)
    out_shape = (rows, rows, NLAG) if last else acc_shape
    return pl.pallas_call(
        functools.partial(correlate_kernel, scaling, first, last),
        grid=(segments // 4,),
        in_specs=in_specs,
        out_specs=full(out_shape),
        out_shape=jax.ShapeDtypeStruct(out_shape, jnp.float32),
        scratch_shapes=[
            pltpu.VMEM(acc_shape, jnp.float32),
            pltpu.VMEM((32 * 40, LANES), jnp.float32),
            pltpu.VMEM((32 * 40, LANES), jnp.float32),
            pltpu.VMEM((NLAG, rows * rows), jnp.bfloat16),
        ],
        compiler_params=pltpu.CompilerParams(
            dimension_semantics=("arbitrary",), vmem_limit_bytes=VMEM_LIMIT
        ),
        name="correlate",
    )(*operands)


def make_table(length_bins):
    bin_freq = np.float32(FIRST_BIN) + np.arange(length_bins, dtype=np.float32)
    lag_steps = np.arange(NLAG, dtype=np.float32) - np.float32(NLAG // 2)
    angles = np.float32(2.0 * math.pi / SAMPLES) * bin_freq[:, None] * lag_steps[None, :]
    table = np.stack([np.cos(angles), -np.sin(angles)]).reshape(2, length_bins // LANES, 4, 32, NLAG)
    table = table.transpose(1, 4, 2, 0, 3).reshape(length_bins // LANES, NLAG, NLAG)
    return jnp.asarray(table).astype(jnp.bfloat16)


def shifted(block, axis, distance):
    devices = range(lax.axis_size(axis))
    route = [((i - distance) % len(devices), i) for i in devices]
    return lax.ppermute(block, axis, route)


def to_peer(piece, offset):
    if offset == (0, 0):
        return piece
    route = [(2 * y + c, peer_of(y, c, offset)) for y in range(4) for c in range(2)]
    return lax.ppermute(piece, "win", route)


SIZES = (16, 16)


def per_device(spectra, pair_blocks):
    length_bins = spectra.shape[3]
    members = lax.axis_size("win")
    block_count = lax.axis_size("chan")
    centre = lax.axis_index("chan")
    member = lax.axis_index("win").astype(jnp.int32)
    reach = pair_blocks.shape[0] * members // 2
    scaling = 1.0 / math.sqrt(spectra.shape[1] * members * length_bins)
    table = make_table(length_bins)

    rows_all = lax.all_gather(pair_blocks, "win", axis=0, tiled=True)
    slot_index = jnp.mod(rows_all - centre + (reach - 1), block_count)

    total = None
    start = 0
    for chunk, own in enumerate(whiten(spectra, SIZES)):
        below, above = own, own
        lower, upper = [], []
        for k in range(1, reach + 1):
            above = shifted(above, "chan", -1)
            upper.append(above)
            if k < reach:
                below = shifted(below, "chan", 1)
                lower.append(below)
        pieces = select_blocks(member[None], slot_index, lower[::-1] + [own] + upper)
        arrived = [to_peer(piece, offset) for piece, offset in zip(pieces, PEERS)]
        steps = SIZES[chunk] // 4
        last = chunk == len(SIZES) - 1
        total = correlate(arrived, table[start : start + steps], total, last, scaling)
        start += steps
    return total[None]


def solution(mesh):
    in_specs = (P(None, "win", "chan", None), P(("chan", "win"), None))
    out_specs = P(("chan", "win"), None, None, None)
    return jax.shard_map(
        per_device, mesh=mesh, in_specs=in_specs, out_specs=out_specs, check_vma=False
    )
```

```python
import functools
import math

import jax
import jax.numpy as jnp
import numpy as np
from jax import lax
from jax.experimental import pallas as pl
from jax.experimental.pallas import tpu as pltpu
from jax.sharding import PartitionSpec as P

NLAG = 256
HALF_BAND = 64
EPS = 1e-05
FIRST_BIN = 60.0
SAMPLES = 15000.0
LANES = 128
VMEM_LIMIT = 56 * 1024 * 1024


def place(segment, sizes):
    chunk = 0
    while segment >= sizes[chunk]:
        segment -= sizes[chunk]
        chunk += 1
    return chunk, segment


def whiten_kernel(spec_ref, *out_refs):
    _, windows, rows, bins = spec_ref.shape
    width = bins + LANES
    bin_pos = lax.broadcasted_iota(jnp.int32, (1, bins), 1)
    count = (
        jnp.minimum(bin_pos + HALF_BAND, bins - 1) - jnp.maximum(bin_pos - HALF_BAND, 0) + 1
    ).astype(jnp.float32)
    lane = lax.broadcasted_iota(jnp.int32, (1, LANES), 1)
    even32 = (lane // 32) % 2 == 0
    even64 = (lane // 64) % 2 == 0
    parts = {}
    for w in range(windows):
        real = spec_ref[0, w].astype(jnp.float32)
        imag = spec_ref[1, w].astype(jnp.float32)
        power = real * real + imag * imag
        padded = jnp.concatenate([power, jnp.zeros((rows, LANES), jnp.float32)], axis=1)
        total = padded
        step = 1
        while step < 2 * HALF_BAND:
            total = total + pltpu.roll(total, width - step, 1)
            step *= 2
        window_sum = pltpu.roll(total, HALF_BAND, 1) + pltpu.roll(padded, width - HALF_BAND, 1)
        factor = lax.rsqrt(window_sum[:, :bins] / count + EPS)
        parts[0, w] = real * factor
        parts[1, w] = imag * factor
    arrays = [parts[r, w] for r in range(2) for w in range(windows)]
    for b in range(bins // LANES):
        v = [a[:, b * LANES : (b + 1) * LANES] for a in arrays]
        for lo, hi in ((0, 1), (2, 3)):
            x, y = v[lo], v[hi]
            v[lo] = jnp.where(even32, x, pltpu.roll(y, 32, 1))
            v[hi] = jnp.where(even32, pltpu.roll(x, LANES - 32, 1), y)
        for lo, hi in ((0, 2), (1, 3)):
            x, y = v[lo], v[hi]
            v[lo] = jnp.where(even64, x, pltpu.roll(y, 64, 1))
            v[hi] = jnp.where(even64, pltpu.roll(x, LANES - 64, 1), y)
        for s in range(4):
            chunk, at = place(4 * b + s, [o.shape[0] for o in out_refs])
            out_refs[chunk][at] = v[s].astype(jnp.bfloat16)


def whiten(spectra, sizes):
    rows = spectra.shape[2]
    return pl.pallas_call(
        whiten_kernel,
        out_shape=[jax.ShapeDtypeStruct((n, rows, LANES), jnp.bfloat16) for n in sizes],
        compiler_params=pltpu.CompilerParams(vmem_limit_bytes=VMEM_LIMIT),
        name="whiten",
    )(spectra)


PEERS = [(0, 0), (2, 0), (2, 1), (1, 0), (3, 0), (1, 1), (3, 1), (0, 1)]


def peer_of(chip, core, offset):
    return (chip + offset[0]) % 4 * 2 + (core + offset[1]) % 2


def select_kernel(block_count, place_ref, idx_ref, *refs):
    blocks, outs, sem = refs[:block_count], refs[block_count:-1], refs[-1]
    member = place_ref[0]
    chip, core = member // 2, member % 2
    for out_ref, offset in zip(outs, PEERS):
        dest = peer_of(chip, core, offset)
        for s in range(2):
            wanted = idx_ref[dest, s]
            for b in range(block_count):

                @pl.when(wanted == b)
                def _():
                    pltpu.make_async_copy(blocks[b], out_ref.at[s], sem).start()

    for out_ref in outs:
        pltpu.make_async_copy(out_ref, out_ref, sem).wait()


def select_blocks(member, slot_index, blocks):
    shape = jax.ShapeDtypeStruct((2,) + blocks[0].shape, blocks[0].dtype)
    return pl.pallas_call(
        functools.partial(select_kernel, len(blocks)),
        in_specs=[pl.BlockSpec(memory_space=pltpu.SMEM)] * 2
        + [pl.BlockSpec(memory_space=pltpu.VMEM)] * len(blocks),
        out_specs=[pl.BlockSpec(memory_space=pl.ANY)] * len(PEERS),
        out_shape=[shape] * len(PEERS),
        scratch_shapes=[pltpu.SemaphoreType.DMA],
        compiler_params=pltpu.CompilerParams(vmem_limit_bytes=VMEM_LIMIT),
        name="select",
    )(member, slot_index, *blocks)


def merge_sources(refs, slot, s, lane):
    v = [ref[slot, s] for ref in refs]
    for bit, width in ((1, 4), (2, 8), (4, 16)):
        even = (lane // width) % 2 == 0
        for lo in range(8):
            if lo & bit:
                continue
            hi = lo | bit
            x, y = v[lo], v[hi]
            v[lo] = jnp.where(even, x, pltpu.roll(y, width, 1))
            v[hi] = jnp.where(even, pltpu.roll(x, LANES - width, 1), y)
    return v


def correlate_kernel(scaling, first, last, *refs):
    sources, refs = refs[:8], refs[8:]
    if first:
        table_ref, mask_ref, out_ref, acc_ref, real_ref, imag_ref, cross_ref = refs
    else:
        table_ref, mask_ref, prior_ref, out_ref, acc_ref, real_ref, imag_ref, cross_ref = refs
    step = pl.program_id(0)
    rows = sources[0].shape[2]
    half = rows // 2
    pitch = real_ref.shape[0] // 32
    lane = lax.broadcasted_iota(jnp.int32, (1, LANES), 1)
    low = lane < 64
    zero = jnp.zeros((LANES, LANES), jnp.bfloat16)

    for s in range(4):
        left = merge_sources(sources, 0, s, lane)
        right = merge_sources(sources, 1, s, lane)
        for h in range(8):
            a = jnp.concatenate([left[h][:half], left[h][half:]], axis=1)
            b = right[h]
            flipped = jnp.concatenate([b, b], axis=0).T
            top = jnp.where(low, flipped, zero)
            bottom = jnp.where(low, zero, flipped)
            weights = jnp.concatenate(
                [
                    jnp.concatenate([top, bottom], axis=0),
                    jnp.concatenate([-top[64:], top[:64], -bottom[64:], bottom[:64]], axis=0),
                ],
                axis=1,
            )
            lhs = jnp.concatenate([a * mask_ref[m] for m in range(4)], axis=0)
            res = lax.dot_general(
                lhs, weights, (((1,), (0,)), ((), ())), preferred_element_type=jnp.float32
            )
            for m in range(4):
                at = pl.ds((4 * h + m) * pitch, half)
                real_ref[at, :] = res[m * half : (m + 1) * half, :LANES]
                imag_ref[at, :] = res[m * half : (m + 1) * half, LANES:]
        for p in range(half):
            cols = pl.ds(LANES * p, LANES)
            real = real_ref[pl.ds(p, 32, stride=pitch), :]
            imag = imag_ref[pl.ds(p, 32, stride=pitch), :]
            cross_ref[pl.ds(64 * s, 32), cols] = real.astype(jnp.bfloat16)
            cross_ref[pl.ds(64 * s + 32, 32), cols] = imag.astype(jnp.bfloat16)
    part = jnp.dot(table_ref[0], cross_ref[...], preferred_element_type=jnp.float32)

    @pl.when(step == 0)
    def _():
        if first:
            acc_ref[...] = part
        else:
            acc_ref[...] = prior_ref[...] + part

    @pl.when(step > 0)
    def _():
        acc_ref[...] += part

    @pl.when(step == pl.num_programs(0) - 1)
    def _():
        if last:
            for p in range(half):
                tile = acc_ref[:, pl.ds(LANES * p, LANES)].T * scaling
                out_ref[p] = tile[:rows]
                out_ref[p + half] = tile[rows:]
        else:
            out_ref[...] = acc_ref[...]


def correlate(pieces, table, prior, last, scaling):
    _, segments, rows, _ = pieces[0].shape
    first = prior is None
    acc_shape = (NLAG, rows * rows)
    lanes = np.arange(2 * LANES) % 4
    masks = np.stack([np.tile(lanes == m, (rows // 2, 1)) for m in range(4)])
    masks = jnp.asarray(masks.astype(np.float32)).astype(jnp.bfloat16)
    full = lambda shape: pl.BlockSpec(
        shape, lambda i: (0,) * len(shape), pipeline_mode=pl.Buffered(1)
    )
    in_specs = [pl.BlockSpec((2, 4, rows, LANES), lambda i: (0, i, 0, 0))] * len(pieces)
    in_specs += [pl.BlockSpec((1, NLAG, NLAG), lambda i: (i, 0, 0)), full(masks.shape)]
    operands = list(pieces) + [table, masks]
    if not first:
        in_specs.append(full(acc_shape))
        operands.append(prior)
    out_shape = (rows, rows, NLAG) if last else acc_shape
    return pl.pallas_call(
        functools.partial(correlate_kernel, scaling, first, last),
        grid=(segments // 4,),
        in_specs=in_specs,
        out_specs=full(out_shape),
        out_shape=jax.ShapeDtypeStruct(out_shape, jnp.float32),
        scratch_shapes=[
            pltpu.VMEM(acc_shape, jnp.float32),
            pltpu.VMEM((32 * 36, LANES), jnp.float32),
            pltpu.VMEM((32 * 36, LANES), jnp.float32),
            pltpu.VMEM((NLAG, rows * rows), jnp.bfloat16),
        ],
        compiler_params=pltpu.CompilerParams(
            dimension_semantics=("arbitrary",), vmem_limit_bytes=VMEM_LIMIT
        ),
        name="correlate",
    )(*operands)


def make_table(length_bins):
    bin_freq = np.float32(FIRST_BIN) + np.arange(length_bins, dtype=np.float32)
    lag_steps = np.arange(NLAG, dtype=np.float32) - np.float32(NLAG // 2)
    angles = np.float32(2.0 * math.pi / SAMPLES) * bin_freq[:, None] * lag_steps[None, :]
    table = np.stack([np.cos(angles), -np.sin(angles)]).reshape(2, length_bins // LANES, 4, 32, NLAG)
    table = table.transpose(1, 4, 2, 0, 3).reshape(length_bins // LANES, NLAG, NLAG)
    return jnp.asarray(table).astype(jnp.bfloat16)


def shifted(block, axis, distance):
    devices = range(lax.axis_size(axis))
    route = [((i - distance) % len(devices), i) for i in devices]
    return lax.ppermute(block, axis, route)


def to_peer(piece, offset):
    if offset == (0, 0):
        return piece
    route = [(2 * y + c, peer_of(y, c, offset)) for y in range(4) for c in range(2)]
    return lax.ppermute(piece, "win", route)


SIZES = (16, 16)


def per_device(spectra, pair_blocks):
    length_bins = spectra.shape[3]
    members = lax.axis_size("win")
    block_count = lax.axis_size("chan")
    centre = lax.axis_index("chan")
    member = lax.axis_index("win").astype(jnp.int32)
    reach = pair_blocks.shape[0] * members // 2
    scaling = 1.0 / math.sqrt(spectra.shape[1] * members * length_bins)
    table = make_table(length_bins)

    rows_all = lax.all_gather(pair_blocks, "win", axis=0, tiled=True)
    slot_index = jnp.mod(rows_all - centre + (reach - 1), block_count)

    total = None
    start = 0
    for chunk, own in enumerate(whiten(spectra, SIZES)):
        below, above = own, own
        lower, upper = [], []
        for k in range(1, reach + 1):
            above = shifted(above, "chan", -1)
            upper.append(above)
            if k < reach:
                below = shifted(below, "chan", 1)
                lower.append(below)
        pieces = select_blocks(member[None], slot_index, lower[::-1] + [own] + upper)
        arrived = [to_peer(piece, offset) for piece, offset in zip(pieces, PEERS)]
        steps = SIZES[chunk] // 4
        last = chunk == len(SIZES) - 1
        total = correlate(arrived, table[start : start + steps], total, last, scaling)
        start += steps
    return total[None]


def solution(mesh):
    in_specs = (P(None, "win", "chan", None), P(("chan", "win"), None))
    out_specs = P(("chan", "win"), None, None, None)
    return jax.shard_map(
        per_device, mesh=mesh, in_specs=in_specs, out_specs=out_specs, check_vma=False
    )
```

```python
import functools
import math

import jax
import jax.numpy as jnp
import numpy as np
from jax import lax
from jax.experimental import pallas as pl
from jax.experimental.pallas import tpu as pltpu
from jax.sharding import PartitionSpec as P

NLAG = 256
HALF_BAND = 64
EPS = 1e-05
FIRST_BIN = 60.0
SAMPLES = 15000.0
LANES = 128
VMEM_LIMIT = 56 * 1024 * 1024


def place(segment, sizes):
    chunk = 0
    while segment >= sizes[chunk]:
        segment -= sizes[chunk]
        chunk += 1
    return chunk, segment


def whiten_kernel(spec_ref, *out_refs):
    _, windows, rows, bins = spec_ref.shape
    width = bins + LANES
    bin_pos = lax.broadcasted_iota(jnp.int32, (1, bins), 1)
    count = (
        jnp.minimum(bin_pos + HALF_BAND, bins - 1) - jnp.maximum(bin_pos - HALF_BAND, 0) + 1
    ).astype(jnp.float32)
    lane = lax.broadcasted_iota(jnp.int32, (1, LANES), 1)
    even32 = (lane // 32) % 2 == 0
    even64 = (lane // 64) % 2 == 0
    parts = {}
    for w in range(windows):
        real = spec_ref[0, w].astype(jnp.float32)
        imag = spec_ref[1, w].astype(jnp.float32)
        power = real * real + imag * imag
        padded = jnp.concatenate([power, jnp.zeros((rows, LANES), jnp.float32)], axis=1)
        total = padded
        step = 1
        while step < 2 * HALF_BAND:
            total = total + pltpu.roll(total, width - step, 1)
            step *= 2
        window_sum = pltpu.roll(total, HALF_BAND, 1) + pltpu.roll(padded, width - HALF_BAND, 1)
        factor = lax.rsqrt(window_sum[:, :bins] / count + EPS)
        parts[0, w] = real * factor
        parts[1, w] = imag * factor
    arrays = [parts[r, w] for r in range(2) for w in range(windows)]
    for b in range(bins // LANES):
        v = [a[:, b * LANES : (b + 1) * LANES] for a in arrays]
        for lo, hi in ((0, 1), (2, 3)):
            x, y = v[lo], v[hi]
            v[lo] = jnp.where(even32, x, pltpu.roll(y, 32, 1))
            v[hi] = jnp.where(even32, pltpu.roll(x, LANES - 32, 1), y)
        for lo, hi in ((0, 2), (1, 3)):
            x, y = v[lo], v[hi]
            v[lo] = jnp.where(even64, x, pltpu.roll(y, 64, 1))
            v[hi] = jnp.where(even64, pltpu.roll(x, LANES - 64, 1), y)
        for s in range(4):
            chunk, at = place(4 * b + s, [o.shape[0] for o in out_refs])
            out_refs[chunk][at] = v[s].astype(jnp.bfloat16)


def whiten(spectra, sizes):
    rows = spectra.shape[2]
    return pl.pallas_call(
        whiten_kernel,
        out_shape=[jax.ShapeDtypeStruct((n, rows, LANES), jnp.bfloat16) for n in sizes],
        compiler_params=pltpu.CompilerParams(vmem_limit_bytes=VMEM_LIMIT),
        name="whiten",
    )(spectra)


PEERS = [(0, 0), (2, 0), (1, 0), (3, 0), (2, 1), (1, 1), (3, 1), (0, 1)]


def peer_of(chip, core, offset):
    return (chip + offset[0]) % 4 * 2 + (core + offset[1]) % 2


def select_kernel(block_count, place_ref, idx_ref, *refs):
    blocks, outs, sem = refs[:block_count], refs[block_count:-1], refs[-1]
    member = place_ref[0]
    chip, core = member // 2, member % 2
    for out_ref, offset in zip(outs, PEERS):
        dest = peer_of(chip, core, offset)
        for s in range(2):
            wanted = idx_ref[dest, s]
            for b in range(block_count):

                @pl.when(wanted == b)
                def _():
                    pltpu.make_async_copy(blocks[b], out_ref.at[s], sem).start()

    for out_ref in outs:
        pltpu.make_async_copy(out_ref, out_ref, sem).wait()


def select_blocks(member, slot_index, blocks):
    shape = jax.ShapeDtypeStruct((2,) + blocks[0].shape, blocks[0].dtype)
    return pl.pallas_call(
        functools.partial(select_kernel, len(blocks)),
        in_specs=[pl.BlockSpec(memory_space=pltpu.SMEM)] * 2
        + [pl.BlockSpec(memory_space=pltpu.VMEM)] * len(blocks),
        out_specs=[pl.BlockSpec(memory_space=pl.ANY)] * len(PEERS),
        out_shape=[shape] * len(PEERS),
        scratch_shapes=[pltpu.SemaphoreType.DMA],
        compiler_params=pltpu.CompilerParams(vmem_limit_bytes=VMEM_LIMIT),
        name="select",
    )(member, slot_index, *blocks)


def merge_sources(refs, slot, s, lane):
    v = [ref[slot, s] for ref in refs]
    for bit, width in ((1, 4), (2, 8), (4, 16)):
        even = (lane // width) % 2 == 0
        for lo in range(8):
            if lo & bit:
                continue
            hi = lo | bit
            x, y = v[lo], v[hi]
            v[lo] = jnp.where(even, x, pltpu.roll(y, width, 1))
            v[hi] = jnp.where(even, pltpu.roll(x, LANES - width, 1), y)
    return v


def correlate_kernel(scaling, first, last, *refs):
    sources, refs = refs[:8], refs[8:]
    if first:
        table_ref, mask_ref, out_ref, acc_ref, real_ref, imag_ref, cross_ref = refs
    else:
        table_ref, mask_ref, prior_ref, out_ref, acc_ref, real_ref, imag_ref, cross_ref = refs
    step = pl.program_id(0)
    rows = sources[0].shape[2]
    half = rows // 2
    pitch = real_ref.shape[0] // 32
    lane = lax.broadcasted_iota(jnp.int32, (1, LANES), 1)
    low = lane < 64
    zero = jnp.zeros((LANES, LANES), jnp.bfloat16)

    for s in range(4):
        left = merge_sources(sources, 0, s, lane)
        right = merge_sources(sources, 1, s, lane)
        for h in range(8):
            a = jnp.concatenate([left[h][:half], left[h][half:]], axis=1)
            b = right[h]
            flipped = jnp.concatenate([b, b], axis=0).T
            top = jnp.where(low, flipped, zero)
            bottom = jnp.where(low, zero, flipped)
            weights = jnp.concatenate(
                [
                    jnp.concatenate([top, bottom], axis=0),
                    jnp.concatenate([-top[64:], top[:64], -bottom[64:], bottom[:64]], axis=0),
                ],
                axis=1,
            )
            lhs = jnp.concatenate([a * mask_ref[m] for m in range(4)], axis=0)
            res = lax.dot_general(
                lhs, weights, (((1,), (0,)), ((), ())), preferred_element_type=jnp.float32
            )
            for m in range(4):
                at = pl.ds((4 * h + m) * pitch, half)
                real_ref[at, :] = res[m * half : (m + 1) * half, :LANES]
                imag_ref[at, :] = res[m * half : (m + 1) * half, LANES:]
        for p in range(half):
            cols = pl.ds(LANES * p, LANES)
            real = real_ref[pl.ds(p, 32, stride=pitch), :]
            imag = imag_ref[pl.ds(p, 32, stride=pitch), :]
            cross_ref[pl.ds(64 * s, 32), cols] = real.astype(jnp.bfloat16)
            cross_ref[pl.ds(64 * s + 32, 32), cols] = imag.astype(jnp.bfloat16)
    part = jnp.dot(table_ref[0], cross_ref[...], preferred_element_type=jnp.float32)

    @pl.when(step == 0)
    def _():
        if first:
            acc_ref[...] = part
        else:
            acc_ref[...] = prior_ref[...] + part

    @pl.when(step > 0)
    def _():
        acc_ref[...] += part

    @pl.when(step == pl.num_programs(0) - 1)
    def _():
        if last:
            for p in range(half):
                tile = acc_ref[:, pl.ds(LANES * p, LANES)].T * scaling
                out_ref[p] = tile[:rows]
                out_ref[p + half] = tile[rows:]
        else:
            out_ref[...] = acc_ref[...]


def correlate(pieces, table, prior, last, scaling):
    _, segments, rows, _ = pieces[0].shape
    first = prior is None
    acc_shape = (NLAG, rows * rows)
    lanes = np.arange(2 * LANES) % 4
    masks = np.stack([np.tile(lanes == m, (rows // 2, 1)) for m in range(4)])
    masks = jnp.asarray(masks.astype(np.float32)).astype(jnp.bfloat16)
    full = lambda shape: pl.BlockSpec(
        shape, lambda i: (0,) * len(shape), pipeline_mode=pl.Buffered(1)
    )
    in_specs = [pl.BlockSpec((2, 4, rows, LANES), lambda i: (0, i, 0, 0))] * len(pieces)
    in_specs += [pl.BlockSpec((1, NLAG, NLAG), lambda i: (i, 0, 0)), full(masks.shape)]
    operands = list(pieces) + [table, masks]
    if not first:
        in_specs.append(full(acc_shape))
        operands.append(prior)
    out_shape = (rows, rows, NLAG) if last else acc_shape
    return pl.pallas_call(
        functools.partial(correlate_kernel, scaling, first, last),
        grid=(segments // 4,),
        in_specs=in_specs,
        out_specs=full(out_shape),
        out_shape=jax.ShapeDtypeStruct(out_shape, jnp.float32),
        scratch_shapes=[
            pltpu.VMEM(acc_shape, jnp.float32),
            pltpu.VMEM((32 * 36, LANES), jnp.float32),
            pltpu.VMEM((32 * 36, LANES), jnp.float32),
            pltpu.VMEM((NLAG, rows * rows), jnp.bfloat16),
        ],
        compiler_params=pltpu.CompilerParams(
            dimension_semantics=("arbitrary",), vmem_limit_bytes=VMEM_LIMIT
        ),
        name="correlate",
    )(*operands)


def make_table(length_bins):
    bin_freq = np.float32(FIRST_BIN) + np.arange(length_bins, dtype=np.float32)
    lag_steps = np.arange(NLAG, dtype=np.float32) - np.float32(NLAG // 2)
    angles = np.float32(2.0 * math.pi / SAMPLES) * bin_freq[:, None] * lag_steps[None, :]
    table = np.stack([np.cos(angles), -np.sin(angles)]).reshape(2, length_bins // LANES, 4, 32, NLAG)
    table = table.transpose(1, 4, 2, 0, 3).reshape(length_bins // LANES, NLAG, NLAG)
    return jnp.asarray(table).astype(jnp.bfloat16)


def shifted(block, axis, distance):
    devices = range(lax.axis_size(axis))
    route = [((i - distance) % len(devices), i) for i in devices]
    return lax.ppermute(block, axis, route)


def to_peer(piece, offset):
    if offset == (0, 0):
        return piece
    route = [(2 * y + c, peer_of(y, c, offset)) for y in range(4) for c in range(2)]
    return lax.ppermute(piece, "win", route)


SIZES = (16, 16)


def per_device(spectra, pair_blocks):
    length_bins = spectra.shape[3]
    members = lax.axis_size("win")
    block_count = lax.axis_size("chan")
    centre = lax.axis_index("chan")
    member = lax.axis_index("win").astype(jnp.int32)
    reach = pair_blocks.shape[0] * members // 2
    scaling = 1.0 / math.sqrt(spectra.shape[1] * members * length_bins)
    table = make_table(length_bins)

    rows_all = lax.all_gather(pair_blocks, "win", axis=0, tiled=True)
    slot_index = jnp.mod(rows_all - centre + (reach - 1), block_count)

    total = None
    start = 0
    for chunk, own in enumerate(whiten(spectra, SIZES)):
        below, above = own, own
        lower, upper = [], []
        for k in range(1, reach + 1):
            above = shifted(above, "chan", -1)
            upper.append(above)
            if k < reach:
                below = shifted(below, "chan", 1)
                lower.append(below)
        pieces = select_blocks(member[None], slot_index, lower[::-1] + [own] + upper)
        arrived = [to_peer(piece, offset) for piece, offset in zip(pieces, PEERS)]
        steps = SIZES[chunk] // 4
        last = chunk == len(SIZES) - 1
        total = correlate(arrived, table[start : start + steps], total, last, scaling)
        start += steps
    return total[None]


def solution(mesh):
    in_specs = (P(None, "win", "chan", None), P(("chan", "win"), None))
    out_specs = P(("chan", "win"), None, None, None)
    return jax.shard_map(
        per_device, mesh=mesh, in_specs=in_specs, out_specs=out_specs, check_vma=False
    )
```
